32 devices in a mesh: gx: 16 (over z, x, core), gy: 2 (over y).
Axes of the slice: x: 2, y: 2, z: 4, core: 2. Of those that a mesh axis runs over, the one named last changes fastest.
Arguments:
- flexibility: bfloat16 [16, 2, 2048, 2048], P('gx', 'gy'), may hold values from -8 to 8
- loads: bfloat16 [16, 2, 192, 2048], P('gx', 'gy'), may hold values from -30 to 30
- dof_order: int32 [16, 2, 2048], P('gx', 'gy'), may hold values from 0 to 2047, each once within a row
- coarse_ids: int32 [16, 2, 128], P('gx', 'gy'), may hold values from 0 to 127, each once within a row
Outputs:
- field: float32 [16, 2, 192, 2048], P('gx', 'gy')
- multipliers: float32 [16, 2, 192, 2048], P('gx', 'gy')
The draws below stay inside these ranges and needn't reach their ends.
All inputs are finite; a program needn't handle non-finite values.
Results may differ from the reference program's by a relative error of at most 0.0038.
Values may be sent and summed in bfloat16 or wider, within the bound.
A program may use at most 64 MiB of HBM per device.

```python
import math
import jax
import jax.numpy as jnp
from jax import lax

ORDER = 2048
FACE = 320
CORN = 128
CPT = 32
RHS = 192
ITERS = 2
NSX = 16
NSY = 2


LOAD_LEVEL = 0.15


def draw_flexibility(key, part):
    first, second, third = jax.random.split(key, 3)
    keys = jax.random.split(first, NSX * NSY)
    diagonal = jax.random.uniform(second, (NSX * NSY, ORDER), jnp.float32, 1.5, 3.0)
    stiffness = jnp.exp(jax.random.uniform(third, (NSX * NSY,), jnp.float32, math.log(0.5), math.log(2.0)))
    eye = jnp.eye(ORDER, dtype=jnp.float32)

    def one_matrix(triple):
        base = jax.random.normal(triple[0], (ORDER, ORDER), jnp.float32)
        sym = (base + base.T) * (0.5 / math.sqrt(2.0 * ORDER))
        matrix = sym * (1.0 - eye) + triple[1][:, None] * eye
        return (matrix * triple[2]).astype(jnp.bfloat16)
    return lax.map(one_matrix, (keys, diagonal, stiffness)).reshape(NSX, NSY, ORDER, ORDER)


def draw_loads(key, part):
    first, second = jax.random.split(key, 2)
    ramp_x = jnp.exp(jnp.arange(NSX, dtype=jnp.float32) * (math.log(3.0) / (NSX - 1)))
    ramp_y = jnp.exp(jnp.arange(NSY, dtype=jnp.float32) * (math.log(3.0) / (NSY - 1)))
    ramp = ramp_x[:, None, None, None] * ramp_y[None, :, None, None]
    base = jnp.clip(jax.random.normal(first, (NSX, NSY, RHS, ORDER), jnp.float32), -4.0, 4.0)
    local = jnp.exp(jax.random.uniform(second, (NSX, NSY, 1, 1), jnp.float32, -math.log(4.0), math.log(4.0)))
    values = base * local
    return (values * ramp * LOAD_LEVEL).astype(jnp.bfloat16)


def setup_inputs(seed: int = 0) -> dict:
    key_of = jax.random.split(jax.random.key(seed), 5)
    flexibility = draw_flexibility(jax.random.fold_in(key_of[4], 71), 0)
    loads = draw_loads(jax.random.fold_in(key_of[4], 71), 0)
    dof_order = jax.vmap(lambda own: jax.random.permutation(own, ORDER))(jax.random.split(key_of[2], NSX * NSY)).reshape((NSX, NSY, ORDER)).astype(jnp.int32)
    coarse_ids = jax.vmap(lambda own: jax.random.permutation(own, CORN))(jax.random.split(key_of[3], NSX * NSY)).reshape((NSX, NSY, CORN)).astype(jnp.int32)
    return dict(flexibility=flexibility, loads=loads, dof_order=dof_order, coarse_ids=coarse_ids)


RHO = 0.2
RHO_CORNER = 0.5
EPS = 1e-06
ROUNDS = ((0, 1, 0), (0, 1, 1), (1, 1, 0), (1, 1, 1), (0, 2, 0), (0, 2, 2))

def partner_of(trace, axis, dist, offset):
    count = trace.shape[axis]
    index = jnp.arange(count)
    lower = (index - offset) // dist % 2 == 0
    above = jnp.roll(trace, -dist, axis)
    below = jnp.roll(trace, dist, axis)
    if axis == 0:
        above = jnp.where((index < count - dist)[:, None, None, None], above, jnp.zeros_like(above))
        below = jnp.where((index >= dist)[:, None, None, None], below, jnp.zeros_like(below))
        return jnp.where(lower[:, None, None, None], above, below)
    return jnp.where(lower[None, :, None, None], above, below)

def cross_averages(slotted):
    first = slotted[..., 0, :]
    second = slotted[..., 1, :]
    third = slotted[..., 2, :]
    fourth = slotted[..., 3, :]
    upper = first + jnp.roll(third, -1, axis=1)
    lower = second + jnp.roll(fourth, -1, axis=1)
    zero = jnp.zeros((1,) + first.shape[1:], jnp.float32)
    cross = jnp.concatenate([zero, upper], axis=0) + jnp.concatenate([lower, zero], axis=0)
    counts = jnp.full((NSX + 1,), 4.0, jnp.float32).at[0].set(2.0).at[NSX].set(2.0)
    means = cross / counts[:, None, None, None]
    slot_a = means[1:]
    slot_b = means[:-1]
    slot_c = jnp.roll(slot_a, 1, axis=1)
    slot_d = jnp.roll(slot_b, 1, axis=1)
    return jnp.stack([slot_a, slot_b, slot_c, slot_d], axis=3)

def reference(flexibility, loads, dof_order, coarse_ids):
    subs = NSX * NSY
    flat_flex = flexibility.reshape(subs, ORDER, ORDER)
    order_full = jnp.broadcast_to(dof_order[:, :, None, :], (NSX, NSY, RHS, ORDER))
    inverse = jnp.argsort(dof_order, axis=-1).astype(jnp.int32)
    inverse_full = jnp.broadcast_to(inverse[:, :, None, :], (NSX, NSY, RHS, ORDER))
    ids_full = jnp.broadcast_to(coarse_ids[:, :, None, :], (NSX, NSY, RHS, CORN))
    slot_inverse = jnp.argsort(coarse_ids, axis=-1).astype(jnp.int32)
    slot_full = jnp.broadcast_to(slot_inverse[:, :, None, :], (NSX, NSY, RHS, CORN))
    multipliers = jnp.zeros((NSX, NSY, RHS, ORDER), jnp.float32)
    field = multipliers
    for step in range(ITERS):
        rhs = (loads.astype(jnp.float32) - multipliers).astype(jnp.bfloat16)

        def solve_one(pair):
            return jnp.dot(pair[0], pair[1], preferred_element_type=jnp.float32)
        field = lax.map(solve_one, (rhs.reshape(subs, RHS, ORDER), flat_flex)).reshape(NSX, NSY, RHS, ORDER)
        ordered = jnp.take_along_axis(field, order_full, axis=3)
        pieces = []
        for r, (axis, dist, offset) in enumerate(ROUNDS):
            own = ordered[..., r * FACE:(r + 1) * FACE]
            other = partner_of(own.astype(jnp.bfloat16), axis, dist, offset)
            pieces.append(RHO * (own - other.astype(jnp.float32)))
        corners = ordered[..., 6 * FACE:]
        slotted = jnp.take_along_axis(corners, slot_full, axis=3).reshape(NSX, NSY, RHS, 4, CPT)
        averaged = cross_averages(slotted).reshape(NSX, NSY, RHS, CORN)
        average = jnp.take_along_axis(averaged, ids_full, axis=3)
        resid = corners - average
        msq = lax.optimization_barrier(jnp.sum(resid * resid, axis=(0, 1, 3))) / (NSX * NSY * CORN)
        scale = 1.0 / jnp.sqrt(msq + EPS)
        pieces.append(RHO_CORNER * resid * scale[None, None, :, None])
        update = jnp.concatenate(pieces, axis=3)
        multipliers = multipliers + jnp.take_along_axis(update, inverse_full, axis=3)
    return (field, multipliers)
```

```python
import functools
import jax
import jax.numpy as jnp
from jax import lax
from jax.experimental import pallas as pl
from jax.experimental.pallas import tpu as pltpu
from jax.sharding import PartitionSpec as P

ITERS = 2
CHUNKS = 1
RHO = 0.2
RHO_CORNER = 0.5
EPS = 1e-06
MESH = pl.DeviceIdType.MESH
ROUNDS = ((0, 1, 0), (0, 1, 1), (1, 1, 0), (1, 1, 1), (0, 2, 0), (0, 2, 2))
BACK = (2, 1, 0)
F32 = jnp.float32
BF16 = jnp.bfloat16


def dot(a, b):
    return jnp.dot(a, b, preferred_element_type=F32)


def dot_nt(a, b):
    return lax.dot_general(a, b, (((1,), (1,)), ((), ())), preferred_element_type=F32)


def split(x):
    hi = x.astype(BF16)
    return hi, (x - hi.astype(F32)).astype(BF16)


def fold(x, low):
    h = x.shape[0] // 2
    lane = lax.broadcasted_iota(jnp.int32, (h, 128), 1)
    top, bottom = x[:h], x[h:]
    if low:
        return jnp.where(lane < 64, top, pltpu.roll(bottom, 64, 1))
    return jnp.where(lane < 64, pltpu.roll(top, 64, 1), bottom)


def unfold(low, high):
    h = low.shape[0]
    lane = lax.broadcasted_iota(jnp.int32, (h, 128), 1)
    top = jnp.where(lane < 64, low, pltpu.roll(high, 64, 1))
    bottom = jnp.where(lane < 64, pltpu.roll(low, 64, 1), high)
    return jnp.concatenate([top, bottom], axis=0)


def kernel(nx, ny, order_hbm, ids_hbm, loads_hbm, flex_hbm, fld, mult,
           order_ref, ids_ref, loads_ref,
           order, flex, perm, permt, cperm, cpermt, fhi, flo, rhs, cmask, xb,
           tb, rv, cs, cr, us, ur, sq, sr, res,
           in_sem, flex_sem, tsend, trecv, csend, crecv, usend, urecv, ssend, srecv):
    rows, n = loads_ref.shape
    face = (n - 128) // 6
    pair_w = 2 * face
    ncorn = ids_ref.shape[1]
    nf = 6 * face
    R = rows // CHUNKS
    h = R // 2
    ix, iy = lax.axis_index("gx"), lax.axis_index("gy")
    ndev = nx * ny
    me = ix * ny + iy
    nch = flex_sem.shape[0]
    cw = n // nch

    order_copy = pltpu.make_async_copy(order_hbm, order_ref, in_sem.at[0])
    ids_copy = pltpu.make_async_copy(ids_hbm, ids_ref, in_sem.at[1])
    loads_copy = pltpu.make_async_copy(loads_hbm, loads_ref, in_sem.at[2])
    order_copy.start()
    ids_copy.start()
    loads_copy.start()

    def flex_copy(c):
        s = pl.ds(c * cw, cw)
        return pltpu.make_async_copy(flex_hbm.at[:, s], flex.at[:, s], flex_sem.at[c])

    for c in range(nch):
        flex_copy(c).start()

    def peer(k):
        p = lax.rem(me + k, ndev)
        return (p // ny, lax.rem(p, ny))

    barrier = pltpu.get_barrier_semaphore()

    def greet(k, carry):
        pl.semaphore_signal(barrier, inc=1, device_id=peer(k), device_id_type=MESH)
        return carry

    lax.fori_loop(1, ndev, greet, 0)

    partners = []
    for axis, dist, off in ROUNDS:
        idx = ix if axis == 0 else iy
        count = nx if axis == 0 else ny
        lower = lax.rem((idx - off + 2 * dist) // dist, 2) == 0
        to = jnp.where(lower, idx + dist, idx - dist)
        if axis == 0:
            partners.append((jnp.logical_and(to >= 0, to < count), (jnp.clip(to, 0, count - 1), iy)))
        else:
            partners.append((None, (ix, lax.rem(to + count, count))))

    for r in range(6):
        present = partners[r][0]
        if present is not None:
            @pl.when(jnp.logical_not(present))
            def _():
                for it in range(ITERS):
                    for c in range(CHUNKS):
                        rv[it, c, r] = jnp.zeros(rv.shape[3:], BF16)

    @pl.when(ix == 0)
    def _():
        for it in range(ITERS):
            for c in range(CHUNKS):
                ur[it, c, 0] = jnp.zeros(ur.shape[3:], F32)

    @pl.when(ix == nx - 1)
    def _():
        for it in range(ITERS):
            for c in range(CHUNKS):
                ur[it, c, 1] = jnp.zeros(ur.shape[3:], F32)

    order_copy.wait()
    for p in range(3):
        base = p * pair_w
        x = jnp.broadcast_to(order_ref[:, base:base + pair_w], (8, pair_w))
        turned = pltpu.roll(x, pair_w - 64, 1)
        low = lax.broadcasted_iota(jnp.int32, (8, 128), 1) < 64
        order[:, base:base + 256] = x[:, :256]
        order[:, base + 256:base + 512] = turned[:, 256:512]
        order[:, base + 512:base + pair_w] = jnp.where(low, x[:, 256:384], x[:, 512:])
    order[:, nf:] = jnp.broadcast_to(order_ref[:, nf:], (8, ncorn))
    step_p = 64

    def build(b, carry):
        base = pl.multiple_of(b * step_p, step_p)
        row = lax.broadcasted_iota(jnp.int32, (step_p, n), 0) + base
        perm[pl.ds(base, step_p), :] = jnp.where(row == order[0:1, :], 1.0, 0.0).astype(BF16)
        return carry

    lax.fori_loop(0, n // step_p, build, 0)
    ids_copy.wait()
    ids = ids_ref[...]
    slot = ids // (ncorn // 4)
    moved = jnp.where(slot == 1, 2, jnp.where(slot == 2, 1, slot))
    ids = moved * (ncorn // 4) + lax.rem(ids, ncorn // 4)
    place = jnp.where(lax.broadcasted_iota(jnp.int32, (ncorn, ncorn), 0) == ids, 1.0, 0.0).astype(BF16)
    cperm[...] = dot_nt(perm[:, nf:], place).astype(BF16)

    def build_t(b0, b1):
        eye = (lax.broadcasted_iota(jnp.int32, (128, 128), 0)
               == lax.broadcasted_iota(jnp.int32, (128, 128), 1))

        def body(b, carry):
            base = pl.multiple_of(b * 128, 128)
            part = order[0:1, pl.ds(base, 128)].astype(F32)
            col = jnp.sum(jnp.where(eye, part, 0.0), axis=1, keepdims=True).astype(jnp.int32)
            hit = lax.broadcasted_iota(jnp.int32, (128, n), 1) == col
            permt[pl.ds(base, 128), :] = jnp.where(hit, 1.0, 0.0).astype(BF16)
            return carry

        lax.fori_loop(b0, b1, body, 0)

    lane = lax.broadcasted_iota(jnp.int32, (R, 128), 1)
    inv_low = jnp.where(ix == nx - 1, 0.5, 0.25).astype(F32)
    inv_high = jnp.where(ix == 0, 0.5, 0.25).astype(F32)
    entries = ndev * ncorn

    def rs(c):
        return slice(c * R, (c + 1) * R)

    def field(it, c):
        for k in range(nch):
            if it == 0 and c == 0:
                flex_copy(k).wait()
            s = slice(k * cw, (k + 1) * cw)
            f = dot(loads_ref[rs(c), :] if it == 0 else rhs[rs(c), :], flex[:, s])
            fld[rs(c), s] = f
            hi, lo = split(f)
            fhi[rs(c), s] = hi
            flo[rs(c), s] = lo

    def y_copy(it, c, k):
        step = (-1, 1)[k] if ny > 2 else 1
        return pltpu.make_async_remote_copy(
            src_ref=cs.at[it, c], dst_ref=cr.at[it, c, k], send_sem=csend.at[it, c, k],
            recv_sem=crecv.at[it, c, k],
            device_id=(ix, lax.rem(iy + step + ny, ny)), device_id_type=MESH)

    ky = 2 if ny > 2 else 1

    def corners(it, c):
        cs[it, c] = dot(fhi[rs(c), :], cperm[...]) + dot(flo[rs(c), :], cperm[...])

    def send_corners(it, c):
        for k in range(ky):
            y_copy(it, c, k).start()

    def face_copy(it, c, r):
        return pltpu.make_async_remote_copy(
            src_ref=tb.at[it, c, r], dst_ref=rv.at[it, c, r], send_sem=tsend.at[it, c, r],
            recv_sem=trecv.at[it, c, r], device_id=partners[r][1], device_id_type=MESH)

    def on(it, c, r, action):
        if partners[r][0] is None:
            action(face_copy(it, c, r))
        else:
            @pl.when(partners[r][0])
            def _():
                action(face_copy(it, c, r))

    def make_pair(it, c, p):
        base = p * pair_w
        t = dot(fhi[rs(c), :], perm[:, base:base + pair_w])
        for q in (0, 1):
            r = 2 * p + q
            tb[it, c, r, :R, :] = t[:, q * 256:q * 256 + 128].astype(BF16)
            tb[it, c, r, R:2 * R, :] = t[:, q * 256 + 128:q * 256 + 256].astype(BF16)
            tb[it, c, r, 2 * R:, :] = fold(t[:, 512:], q == 0).astype(BF16)

    def send(it, c, *faces):
        for r in faces:
            on(it, c, r, lambda d: d.start())

    def side_copy(it, c, k):
        to = jnp.clip(ix + 1 if k == 0 else ix - 1, 0, nx - 1)
        return pltpu.make_async_remote_copy(
            src_ref=us.at[it, c, k], dst_ref=ur.at[it, c, k], send_sem=usend.at[it, c, k],
            recv_sem=urecv.at[it, c, k], device_id=(to, iy), device_id_type=MESH)

    def across(it, c):
        own = cs[it, c]
        fromup, fromdown = cr[it, c, 0], cr[it, c, ky - 1]
        return own + jnp.where(lax.rem(lane, 64) < 32, pltpu.roll(fromup, 96, 1), pltpu.roll(fromdown, 32, 1))

    def send_sides(it, c):
        for k in range(ky):
            y_copy(it, c, k).wait_recv()
        w = across(it, c)
        res[c] = w
        us[it, c, 0] = fold(w, True)
        us[it, c, 1] = fold(w, False)

        @pl.when(ix < nx - 1)
        def _():
            side_copy(it, c, 0).start()

        @pl.when(ix > 0)
        def _():
            side_copy(it, c, 1).start()

    def residual(it, c):
        @pl.when(ix > 0)
        def _():
            side_copy(it, c, 0).wait_recv()

        @pl.when(ix < nx - 1)
        def _():
            side_copy(it, c, 1).wait_recv()

        cross = res[c] + unfold(ur[it, c, 1], ur[it, c, 0])
        resid = cs[it, c] - cross * jnp.where(lane < 64, inv_low, inv_high)
        res[c] = resid
        z = jnp.concatenate([resid * resid, jnp.zeros((-R % 128, 128), F32)], axis=0)
        sq[it, c] = jnp.sum(z.T, axis=0, keepdims=True)

        def spread(k, carry):
            pltpu.make_async_remote_copy(
                src_ref=sq.at[it, c], dst_ref=sr.at[it, c, ndev - 1 - k], send_sem=ssend.at[it, c],
                recv_sem=srecv.at[it, c], device_id=peer(k), device_id_type=MESH).start()
            return carry

        lax.fori_loop(1, ndev, spread, 0)

    def own_part(it, c):
        for k in range(nch):
            s = slice(k * cw, (k + 1) * cw)
            m = cmask[:, s] * fld[rs(c), s]
            mult[rs(c), s] = m if it == 0 else mult[rs(c), s] + m

    def finish(it, c):
        for p in BACK:
            for q in (0, 1):
                on(it, c, 2 * p + q, lambda d: d.wait_recv())
            tails = []
            for q in (0, 1):
                r = 2 * p + q
                base = p * pair_w + q * 256
                xb[:, base:base + 128] = rv[it, c, r, :R, :]
                xb[:, base + 128:base + 256] = rv[it, c, r, R:2 * R, :]
                tails.append(rv[it, c, r, 2 * R:, :].astype(F32))
            xb[:, p * pair_w + 512:(p + 1) * pair_w] = unfold(*tails).astype(BF16)
            w = slice(p * pair_w, (p + 1) * pair_w)
            for k in range(nch):
                s = slice(k * cw, (k + 1) * cw)
                mult[rs(c), s] += -RHO * dot(xb[:, w], permt[w, s])
        pltpu.make_async_copy(sr.at[it, c], sr.at[it, c], srecv.at[it, c]).wait()
        total = sq[it, c] + jnp.sum(sr[it, c], axis=0)
        scale = RHO_CORNER / jnp.sqrt(total / entries + EPS)
        grid = jnp.broadcast_to(scale, (128, R + -R % 128)).T[:R]
        hi, lo = split(res[c] * grid)
        both = jnp.concatenate([hi, lo], axis=1)
        for k in range(nch):
            s = slice(k * cw, (k + 1) * cw)
            cp = cpermt[:, s]
            m = mult[rs(c), s] + dot(both, jnp.concatenate([cp, cp], axis=0))
            mult[rs(c), s] = m
            if it < ITERS - 1:
                rhs[rs(c), s] = (loads_ref[rs(c), s].astype(F32) - m).astype(BF16)

    loads_copy.wait()
    c = 0
    for it in range(ITERS):
        field(it, c)
        corners(it, c)
        if it == 0:
            pl.semaphore_wait(barrier, ndev - 1)
        send_corners(it, c)
        make_pair(it, c, 2)
        send(it, c, 4)
        make_pair(it, c, 1)
        send(it, c, 2, 3)
        make_pair(it, c, 0)
        send(it, c, 0)
        send_sides(it, c)
        send(it, c, 5)
        if it == 0:
            build_t(0, n // 128)
            ct = dot(place, permt[nf:, :])
            cpermt[...] = ct.astype(BF16)
            cmask[...] = RHO * (1.0 - jnp.sum(ct, axis=0, keepdims=True))
        residual(it, c)
        send(it, c, 1)
        own_part(it, c)
        finish(it, c)

    for it in range(ITERS):
        for c in range(CHUNKS):
            for r in range(6):
                on(it, c, r, lambda d: d.wait_send())
            for k in range(ky):
                y_copy(it, c, k).wait_send()

            @pl.when(ix < nx - 1)
            def _():
                side_copy(it, c, 0).wait_send()

            @pl.when(ix > 0)
            def _():
                side_copy(it, c, 1).wait_send()

            pltpu.make_async_copy(sr.at[it, c], sr.at[it, c], ssend.at[it, c]).wait()


def local(nx, ny, flexibility, loads, dof_order, coarse_ids):
    flex = flexibility[0, 0]
    load = loads[0, 0]
    ids = coarse_ids[0]
    rows, n = load.shape
    corners = ids.shape[1]
    face = (n - corners) // 6
    ndev = nx * ny
    R = rows // CHUNKS
    trace_rows = R * face // 128
    vm = pl.BlockSpec(memory_space=pltpu.VMEM)
    hbm = pl.BlockSpec(memory_space=pltpu.HBM)
    sems = pltpu.SemaphoreType.DMA
    ky = 2 if ny > 2 else 1
    out = jax.ShapeDtypeStruct((rows, n), F32)
    ic = (ITERS, CHUNKS)
    field, mult = pl.pallas_call(
        functools.partial(kernel, nx, ny),
        out_shape=(out, out),
        in_specs=[hbm, hbm, hbm, hbm],
        out_specs=(vm, vm),
        scratch_shapes=[
            pltpu.VMEM((1, n), jnp.int32), pltpu.VMEM((1, corners), jnp.int32), pltpu.VMEM((rows, n), BF16),
            pltpu.VMEM((8, n), jnp.int32),
            pltpu.VMEM((n, n), BF16), pltpu.VMEM((n, n), BF16), pltpu.VMEM((n, n), BF16),
            pltpu.VMEM((n, corners), BF16), pltpu.VMEM((corners, n), BF16),
            pltpu.VMEM((rows, n), BF16), pltpu.VMEM((rows, n), BF16), pltpu.VMEM((rows, n), BF16),
            pltpu.VMEM((1, n), F32), pltpu.VMEM((R, 6 * face), BF16),
            pltpu.VMEM(ic + (6, trace_rows, 128), BF16), pltpu.VMEM(ic + (6, trace_rows, 128), BF16),
            pltpu.VMEM(ic + (R, 128), F32), pltpu.VMEM(ic + (ky, R, 128), F32),
            pltpu.VMEM(ic + (2, R // 2, 128), F32), pltpu.VMEM(ic + (2, R // 2, 128), F32),
            pltpu.VMEM(ic + (1, R + -R % 128), F32), pltpu.VMEM(ic + (ndev - 1, 1, R + -R % 128), F32),
            pltpu.VMEM((CHUNKS, R, 128), F32),
            sems((3,)), sems((4,)), sems(ic + (6,)), sems(ic + (6,)), sems(ic + (ky,)), sems(ic + (ky,)),
            sems(ic + (2,)), sems(ic + (2,)), sems(ic), sems(ic),
        ],
        compiler_params=pltpu.CompilerParams(
            collective_id=0, has_side_effects=True, vmem_limit_bytes=48 * 1024 * 1024),
    )(dof_order[0], ids, load, flex)
    return (field[None, None], mult[None, None])


def solution(mesh):
    nx, ny = mesh.shape["gx"], mesh.shape["gy"]
    placed = (
        P("gx", "gy", None, None),
        P("gx", "gy", None, None),
        P("gx", "gy", None),
        P("gx", "gy", None),
    )
    return jax.shard_map(
        functools.partial(local, nx, ny),
        mesh=mesh,
        in_specs=placed,
        out_specs=(P("gx", "gy", None, None), P("gx", "gy", None, None)),
        check_vma=False,
    )
```

```python
import functools
import jax
import jax.numpy as jnp
from jax import lax
from jax.experimental import pallas as pl
from jax.experimental.pallas import tpu as pltpu
from jax.sharding import PartitionSpec as P

ITERS = 2
CHUNKS = 1
RHO = 0.2
RHO_CORNER = 0.5
EPS = 1e-06
MESH = pl.DeviceIdType.MESH
ROUNDS = ((0, 1, 0), (0, 1, 1), (1, 1, 0), (1, 1, 1), (0, 2, 0), (0, 2, 2))
BACK = (2, 1, 0)
F32 = jnp.float32
BF16 = jnp.bfloat16
SIDE = F32


def dot(a, b):
    return jnp.dot(a, b, preferred_element_type=F32)


def dot_nt(a, b):
    return lax.dot_general(a, b, (((1,), (1,)), ((), ())), preferred_element_type=F32)


def split(x):
    hi = x.astype(BF16)
    return hi, (x - hi.astype(F32)).astype(BF16)


def fold(x, low):
    h = x.shape[0] // 2
    lane = lax.broadcasted_iota(jnp.int32, (h, 128), 1)
    top, bottom = x[:h], x[h:]
    if low:
        return jnp.where(lane < 64, top, pltpu.roll(bottom, 64, 1))
    return jnp.where(lane < 64, pltpu.roll(top, 64, 1), bottom)


def unfold(low, high):
    h = low.shape[0]
    lane = lax.broadcasted_iota(jnp.int32, (h, 128), 1)
    top = jnp.where(lane < 64, low, pltpu.roll(high, 64, 1))
    bottom = jnp.where(lane < 64, pltpu.roll(low, 64, 1), high)
    return jnp.concatenate([top, bottom], axis=0)


def kernel(nx, ny, order_hbm, ids_hbm, loads_hbm, flex_hbm, fld, mult,
           order_ref, ids_ref, loads_ref,
           order, flex, perm, permt, cperm, cpermt, fhi, flo, rhs, cmask, xb, fcol,
           tb, rv, cs, cr, us, ur, sq, sr, res,
           in_sem, flex_sem, tsend, trecv, csend, crecv, usend, urecv, ssend, srecv):
    rows, n = loads_ref.shape
    face = (n - 128) // 6
    pair_w = 2 * face
    ncorn = ids_ref.shape[1]
    nf = 6 * face
    R = rows // CHUNKS
    h = R // 2
    ix, iy = lax.axis_index("gx"), lax.axis_index("gy")
    ndev = nx * ny
    me = ix * ny + iy
    nch = flex_sem.shape[0]
    cw = n // nch

    order_copy = pltpu.make_async_copy(order_hbm, order_ref, in_sem.at[0])
    ids_copy = pltpu.make_async_copy(ids_hbm, ids_ref, in_sem.at[1])
    loads_copy = pltpu.make_async_copy(loads_hbm, loads_ref, in_sem.at[2])
    order_copy.start()
    ids_copy.start()
    loads_copy.start()

    def flex_copy(c):
        s = pl.ds(c * cw, cw)
        return pltpu.make_async_copy(flex_hbm.at[:, s], flex.at[:, s], flex_sem.at[c])

    for c in range(nch):
        flex_copy(c).start()

    def peer(k):
        p = lax.rem(me + k, ndev)
        return (p // ny, lax.rem(p, ny))

    barrier = pltpu.get_barrier_semaphore()

    def greet(k, carry):
        pl.semaphore_signal(barrier, inc=1, device_id=peer(k), device_id_type=MESH)
        return carry

    lax.fori_loop(1, ndev, greet, 0)

    partners = []
    for axis, dist, off in ROUNDS:
        idx = ix if axis == 0 else iy
        count = nx if axis == 0 else ny
        lower = lax.rem((idx - off + 2 * dist) // dist, 2) == 0
        to = jnp.where(lower, idx + dist, idx - dist)
        if axis == 0:
            partners.append((jnp.logical_and(to >= 0, to < count), (jnp.clip(to, 0, count - 1), iy)))
        else:
            partners.append((None, (ix, lax.rem(to + count, count))))

    for r in range(6):
        present = partners[r][0]
        if present is not None:
            @pl.when(jnp.logical_not(present))
            def _():
                for it in range(ITERS):
                    for c in range(CHUNKS):
                        rv[it, c, r] = jnp.zeros(rv.shape[3:], BF16)

    @pl.when(ix == 0)
    def _():
        for it in range(ITERS):
            for c in range(CHUNKS):
                ur[it, c, 0] = jnp.zeros(ur.shape[3:], ur.dtype)

    @pl.when(ix == nx - 1)
    def _():
        for it in range(ITERS):
            for c in range(CHUNKS):
                ur[it, c, 1] = jnp.zeros(ur.shape[3:], ur.dtype)

    order_copy.wait()
    for p in range(3):
        base = p * pair_w
        x = jnp.broadcast_to(order_ref[:, base:base + pair_w], (8, pair_w))
        turned = pltpu.roll(x, pair_w - 64, 1)
        low = lax.broadcasted_iota(jnp.int32, (8, 128), 1) < 64
        order[:, base:base + 256] = x[:, :256]
        order[:, base + 256:base + 512] = turned[:, 256:512]
        order[:, base + 512:base + pair_w] = jnp.where(low, x[:, 256:384], x[:, 512:])
    order[:, nf:] = jnp.broadcast_to(order_ref[:, nf:], (8, ncorn))
    step_p = 64

    def build(b, carry):
        base = pl.multiple_of(b * step_p, step_p)
        row = lax.broadcasted_iota(jnp.int32, (step_p, n), 0) + base
        perm[pl.ds(base, step_p), :] = jnp.where(row == order[0:1, :], 1.0, 0.0).astype(BF16)
        return carry

    lax.fori_loop(0, n // step_p, build, 0)
    ids_copy.wait()
    ids = ids_ref[...]
    slot = ids // (ncorn // 4)
    moved = jnp.where(slot == 1, 2, jnp.where(slot == 2, 1, slot))
    ids = moved * (ncorn // 4) + lax.rem(ids, ncorn // 4)
    place = jnp.where(lax.broadcasted_iota(jnp.int32, (ncorn, ncorn), 0) == ids, 1.0, 0.0).astype(BF16)
    cperm[...] = dot_nt(perm[:, nf:], place).astype(BF16)

    def build_t(b0, b1):
        eye = (lax.broadcasted_iota(jnp.int32, (128, 128), 0)
               == lax.broadcasted_iota(jnp.int32, (128, 128), 1))

        def body(b, carry):
            base = pl.multiple_of(b * 128, 128)
            part = order[0:1, pl.ds(base, 128)].astype(F32)
            col = jnp.sum(jnp.where(eye, part, 0.0), axis=1, keepdims=True).astype(jnp.int32)
            hit = lax.broadcasted_iota(jnp.int32, (128, n), 1) == col
            permt[pl.ds(base, 128), :] = jnp.where(hit, 1.0, 0.0).astype(BF16)
            return carry

        lax.fori_loop(b0, b1, body, 0)

    lane = lax.broadcasted_iota(jnp.int32, (R, 128), 1)
    inv_low = jnp.where(ix == nx - 1, 0.5, 0.25).astype(F32)
    inv_high = jnp.where(ix == 0, 0.5, 0.25).astype(F32)
    entries = ndev * ncorn

    def rs(c):
        return slice(c * R, (c + 1) * R)

    def field(it, c):
        for k in range(nch):
            if it == 0 and c == 0:
                flex_copy(k).wait()
            s = slice(k * cw, (k + 1) * cw)
            f = dot(loads_ref[rs(c), :] if it == 0 else rhs[rs(c), :], flex[:, s])
            fld[rs(c), s] = f
            hi, lo = split(f)
            fhi[rs(c), s] = hi
            if it == 0:
                flo[rs(c), s] = lo

    steps = (-1, 1) if ny > 2 else (1,)
    ky = len(steps)

    def y_copy(it, c, k):
        return pltpu.make_async_remote_copy(
            src_ref=cs.at[it, c], dst_ref=cr.at[it, c, k], send_sem=csend.at[it, c, k],
            recv_sem=crecv.at[it, c, k],
            device_id=(ix, lax.rem(iy + steps[k] + ny, ny)), device_id_type=MESH)

    def corners(it, c):
        cs[it, c] = dot(fhi[rs(c), :], cperm[...]) + dot(flo[rs(c), :], cperm[...])

    def face_copy(it, c, r):
        return pltpu.make_async_remote_copy(
            src_ref=tb.at[it, c, r], dst_ref=rv.at[it, c, r], send_sem=tsend.at[it, c, r],
            recv_sem=trecv.at[it, c, r], device_id=partners[r][1], device_id_type=MESH)

    def on(it, c, r, action):
        if partners[r][0] is None:
            action(face_copy(it, c, r))
        else:
            @pl.when(partners[r][0])
            def _():
                action(face_copy(it, c, r))

    def make_pair(it, c, p):
        base = p * pair_w
        t = dot(fhi[rs(c), :], perm[:, base:base + pair_w])
        for q in (0, 1):
            r = 2 * p + q
            tb[it, c, r, :R, :] = t[:, q * 256:q * 256 + 128].astype(BF16)
            tb[it, c, r, R:2 * R, :] = t[:, q * 256 + 128:q * 256 + 256].astype(BF16)
            tb[it, c, r, 2 * R:, :] = fold(t[:, 512:], q == 0).astype(BF16)

    def send(it, c, *faces):
        for r in faces:
            on(it, c, r, lambda d: d.start())

    def side_copy(it, c, k, j):
        to = jnp.clip(ix + 1 if k == 0 else ix - 1, 0, nx - 1)
        toy = iy if j == 0 else lax.rem(iy + steps[j - 1] + ny, ny)
        return pltpu.make_async_remote_copy(
            src_ref=us.at[it, c, k], dst_ref=ur.at[it, c, k, j], send_sem=usend.at[it, c, k, j],
            recv_sem=urecv.at[it, c, k, j], device_id=(to, toy), device_id_type=MESH)

    def on_sides(it, c, action, arriving):
        for k in range(2):
            @pl.when((ix > 0) if (k == 0) == arriving else (ix < nx - 1))
            def _():
                for j in range(1 + ky):
                    action(side_copy(it, c, k, j))

    def send_corners(it, c):
        us[it, c, 0] = fold(cs[it, c], True).astype(us.dtype)
        us[it, c, 1] = fold(cs[it, c], False).astype(us.dtype)
        on_sides(it, c, lambda d: d.start(), False)
        for k in range(ky):
            y_copy(it, c, k).start()

    def residual(it, c):
        for k in range(ky):
            y_copy(it, c, k).wait_recv()
        on_sides(it, c, lambda d: d.wait_recv(), True)

        def column(j):
            own = cs[it, c] if j == 0 else cr[it, c, j - 1]
            return own + unfold(ur[it, c, 1, j].astype(F32), ur[it, c, 0, j].astype(F32))

        cross = column(0) + jnp.where(lax.rem(lane, 64) < 32, pltpu.roll(column(1), 96, 1), pltpu.roll(column(ky), 32, 1))
        resid = cs[it, c] - cross * jnp.where(lane < 64, inv_low, inv_high)
        res[c] = resid
        z = jnp.concatenate([resid * resid, jnp.zeros((-R % 128, 128), F32)], axis=0)
        sq[it, c] = jnp.sum(z.T, axis=0, keepdims=True)

        def spread(k, carry):
            pltpu.make_async_remote_copy(
                src_ref=sq.at[it, c], dst_ref=sr.at[it, c, ndev - 1 - k], send_sem=ssend.at[it, c],
                recv_sem=srecv.at[it, c], device_id=peer(k), device_id_type=MESH).start()
            return carry

        lax.fori_loop(1, ndev, spread, 0)

    def own_part(it, c):
        for k in range(nch):
            s = slice(k * cw, (k + 1) * cw)
            m = cmask[:, s] * fld[rs(c), s]
            mult[rs(c), s] = m if it == 0 else mult[rs(c), s] + m

    def finish(it, c):
        for p in BACK:
            for q in (0, 1):
                on(it, c, 2 * p + q, lambda d: d.wait_recv())
            tails = []
            for q in (0, 1):
                r = 2 * p + q
                base = p * pair_w + q * 256
                xb[:, base:base + 128] = rv[it, c, r, :R, :]
                xb[:, base + 128:base + 256] = rv[it, c, r, R:2 * R, :]
                tails.append(rv[it, c, r, 2 * R:, :].astype(F32))
            xb[:, p * pair_w + 512:(p + 1) * pair_w] = unfold(*tails).astype(BF16)
            w = slice(p * pair_w, (p + 1) * pair_w)
            for k in range(nch):
                s = slice(k * cw, (k + 1) * cw)
                mult[rs(c), s] += -RHO * dot(xb[:, w], permt[w, s])
        pltpu.make_async_copy(sr.at[it, c], sr.at[it, c], srecv.at[it, c]).wait()
        total = sq[it, c] + jnp.sum(sr[it, c], axis=0)
        scale = RHO_CORNER / jnp.sqrt(total / entries + EPS)
        grid = jnp.broadcast_to(scale, (128, R + -R % 128)).T[:R]
        hi, lo = split(res[c] * grid)
        both = jnp.concatenate([hi, lo], axis=1)
        for k in range(nch):
            s = slice(k * cw, (k + 1) * cw)
            cp = cpermt[:, s]
            m = mult[rs(c), s] + dot(both, jnp.concatenate([cp, cp], axis=0))
            mult[rs(c), s] = m
            if it < ITERS - 1:
                rhs[rs(c), s] = (loads_ref[rs(c), s].astype(F32) - m).astype(BF16)

    loads_copy.wait()
    c = 0
    for it in range(ITERS):
        if it > 0:
            cs[it, c] = dot(rhs[...], fcol[...])
            send_corners(it, c)
        field(it, c)
        if it == 0:
            corners(it, c)
            pl.semaphore_wait(barrier, ndev - 1)
            send_corners(it, c)
        make_pair(it, c, 2)
        send(it, c, 4)
        make_pair(it, c, 1)
        send(it, c, 2)
        make_pair(it, c, 0)
        send(it, c, 0)
        residual(it, c)
        send(it, c, 5, 1, 3)
        if it == 0:
            build_t(0, n // 128)
            ct = dot(place, permt[nf:, :])
            cpermt[...] = ct.astype(BF16)
            cmask[...] = RHO * (1.0 - jnp.sum(ct, axis=0, keepdims=True))

            def corner_columns(b, carry):
                base = pl.multiple_of(b * 512, 512)
                fcol[pl.ds(base, 512), :] = dot(flex[pl.ds(base, 512), :], cperm[...]).astype(BF16)
                return carry

            lax.fori_loop(0, n // 512, corner_columns, 0)
        own_part(it, c)
        finish(it, c)

    for it in range(ITERS):
        for c in range(CHUNKS):
            for r in range(6):
                on(it, c, r, lambda d: d.wait_send())
            for k in range(ky):
                y_copy(it, c, k).wait_send()

            on_sides(it, c, lambda d: d.wait_send(), False)
            pltpu.make_async_copy(sr.at[it, c], sr.at[it, c], ssend.at[it, c]).wait()


def store(field, mult, field_hbm, mult_hbm, sem):
    copies = [pltpu.make_async_copy(field, field_hbm, sem.at[0]), pltpu.make_async_copy(mult, mult_hbm, sem.at[1])]
    for c in copies:
        c.start()
    for c in copies:
        c.wait()


def local(nx, ny, flexibility, loads, dof_order, coarse_ids):
    flex = flexibility[0, 0]
    load = loads[0, 0]
    ids = coarse_ids[0]
    rows, n = load.shape
    corners = ids.shape[1]
    face = (n - corners) // 6
    ndev = nx * ny
    R = rows // CHUNKS
    trace_rows = R * face // 128
    vm = pl.BlockSpec(memory_space=pltpu.VMEM)
    hbm = pl.BlockSpec(memory_space=pltpu.HBM)
    sems = pltpu.SemaphoreType.DMA
    ky = 2 if ny > 2 else 1
    out = jax.ShapeDtypeStruct((rows, n), F32)
    ic = (ITERS, CHUNKS)
    field, mult = pl.pallas_call(
        functools.partial(kernel, nx, ny),
        out_shape=(out, out),
        in_specs=[hbm, hbm, hbm, hbm],
        out_specs=(vm, vm),
        scratch_shapes=[
            pltpu.VMEM((1, n), jnp.int32), pltpu.VMEM((1, corners), jnp.int32), pltpu.VMEM((rows, n), BF16),
            pltpu.VMEM((8, n), jnp.int32),
            pltpu.VMEM((n, n), BF16), pltpu.VMEM((n, n), BF16), pltpu.VMEM((n, n), BF16),
            pltpu.VMEM((n, corners), BF16), pltpu.VMEM((corners, n), BF16),
            pltpu.VMEM((rows, n), BF16), pltpu.VMEM((rows, n), BF16), pltpu.VMEM((rows, n), BF16),
            pltpu.VMEM((1, n), F32), pltpu.VMEM((R, 6 * face), BF16), pltpu.VMEM((n, corners), BF16),
            pltpu.VMEM(ic + (6, trace_rows, 128), BF16), pltpu.VMEM(ic + (6, trace_rows, 128), BF16),
            pltpu.VMEM(ic + (R, 128), F32), pltpu.VMEM(ic + (ky, R, 128), F32),
            pltpu.VMEM(ic + (2, R // 2, 128), SIDE), pltpu.VMEM(ic + (2, 1 + ky, R // 2, 128), SIDE),
            pltpu.VMEM(ic + (1, R + -R % 128), F32), pltpu.VMEM(ic + (ndev - 1, 1, R + -R % 128), F32),
            pltpu.VMEM((CHUNKS, R, 128), F32),
            sems((3,)), sems((4,)), sems(ic + (6,)), sems(ic + (6,)), sems(ic + (ky,)), sems(ic + (ky,)),
            sems(ic + (2, 1 + ky)), sems(ic + (2, 1 + ky)), sems(ic), sems(ic),
        ],
        compiler_params=pltpu.CompilerParams(
            collective_id=0, has_side_effects=True, vmem_limit_bytes=48 * 1024 * 1024),
    )(dof_order[0], ids, load, flex)
    field, mult = pl.pallas_call(
        store,
        out_shape=(out, out),
        in_specs=[vm, vm],
        out_specs=(hbm, hbm),
        scratch_shapes=[sems((2,))],
        compiler_params=pltpu.CompilerParams(has_side_effects=True, vmem_limit_bytes=1024 * 1024),
    )(field, mult)
    return (field[None, None], mult[None, None])


def solution(mesh):
    nx, ny = mesh.shape["gx"], mesh.shape["gy"]
    placed = (
        P("gx", "gy", None, None),
        P("gx", "gy", None, None),
        P("gx", "gy", None),
        P("gx", "gy", None),
    )
    return jax.shard_map(
        functools.partial(local, nx, ny),
        mesh=mesh,
        in_specs=placed,
        out_specs=(P("gx", "gy", None, None), P("gx", "gy", None, None)),
        check_vma=False,
    )
```

```python
import functools
import jax
import jax.numpy as jnp
from jax import lax
from jax.experimental import pallas as pl
from jax.experimental.pallas import tpu as pltpu
from jax.sharding import PartitionSpec as P

ITERS = 2
CHUNKS = 1
RHO = 0.2
RHO_CORNER = 0.5
EPS = 1e-06
MESH = pl.DeviceIdType.MESH
ROUNDS = ((0, 1, 0), (0, 1, 1), (1, 1, 0), (1, 1, 1), (0, 2, 0), (0, 2, 2))
BACK = (2, 1, 0)
F32 = jnp.float32
BF16 = jnp.bfloat16
SIDE = F32


def dot(a, b):
    return jnp.dot(a, b, preferred_element_type=F32)


def dot_nt(a, b):
    return lax.dot_general(a, b, (((1,), (1,)), ((), ())), preferred_element_type=F32)


def split(x):
    hi = x.astype(BF16)
    return hi, (x - hi.astype(F32)).astype(BF16)


def fold(x, low):
    h = x.shape[0] // 2
    lane = lax.broadcasted_iota(jnp.int32, (h, 128), 1)
    top, bottom = x[:h], x[h:]
    if low:
        return jnp.where(lane < 64, top, pltpu.roll(bottom, 64, 1))
    return jnp.where(lane < 64, pltpu.roll(top, 64, 1), bottom)


def unfold(low, high):
    h = low.shape[0]
    lane = lax.broadcasted_iota(jnp.int32, (h, 128), 1)
    top = jnp.where(lane < 64, low, pltpu.roll(high, 64, 1))
    bottom = jnp.where(lane < 64, pltpu.roll(low, 64, 1), high)
    return jnp.concatenate([top, bottom], axis=0)


def kernel(nx, ny, order_hbm, ids_hbm, loads_hbm, flex_hbm, fld, mult,
           order_ref, ids_ref, loads_ref,
           order, flex, perm, permt, cperm, cpermt, fhi, flo, rhs, cmask, xb, fcol,
           tb, rv, cs, cr, us, ur, sq, sr, res,
           in_sem, flex_sem, tsend, trecv, csend, crecv, usend, urecv, ssend, srecv):
    rows, n = loads_ref.shape
    face = (n - 128) // 6
    pair_w = 2 * face
    ncorn = ids_ref.shape[1]
    nf = 6 * face
    R = rows // CHUNKS
    h = R // 2
    ix, iy = lax.axis_index("gx"), lax.axis_index("gy")
    ndev = nx * ny
    me = ix * ny + iy
    nch = flex_sem.shape[0]
    cw = n // nch

    order_copy = pltpu.make_async_copy(order_hbm, order_ref, in_sem.at[0])
    ids_copy = pltpu.make_async_copy(ids_hbm, ids_ref, in_sem.at[1])
    loads_copy = pltpu.make_async_copy(loads_hbm, loads_ref, in_sem.at[2])
    order_copy.start()
    ids_copy.start()
    loads_copy.start()

    def flex_copy(c):
        s = pl.ds(c * cw, cw)
        return pltpu.make_async_copy(flex_hbm.at[:, s], flex.at[:, s], flex_sem.at[c])

    for c in range(nch):
        flex_copy(c).start()

    def peer(k):
        p = lax.rem(me + k, ndev)
        return (p // ny, lax.rem(p, ny))

    barrier = pltpu.get_barrier_semaphore()

    def greet(k, carry):
        pl.semaphore_signal(barrier, inc=1, device_id=peer(k), device_id_type=MESH)
        return carry

    lax.fori_loop(1, ndev, greet, 0)

    partners = []
    for axis, dist, off in ROUNDS:
        idx = ix if axis == 0 else iy
        count = nx if axis == 0 else ny
        lower = lax.rem((idx - off + 2 * dist) // dist, 2) == 0
        to = jnp.where(lower, idx + dist, idx - dist)
        if axis == 0:
            partners.append((jnp.logical_and(to >= 0, to < count), (jnp.clip(to, 0, count - 1), iy)))
        else:
            partners.append((None, (ix, lax.rem(to + count, count))))

    for r in range(6):
        present = partners[r][0]
        if present is not None:
            @pl.when(jnp.logical_not(present))
            def _():
                for it in range(ITERS):
                    for c in range(CHUNKS):
                        rv[it, c, r] = jnp.zeros(rv.shape[3:], BF16)

    @pl.when(ix == 0)
    def _():
        for it in range(ITERS):
            for c in range(CHUNKS):
                ur[it, c, 0] = jnp.zeros(ur.shape[3:], ur.dtype)

    @pl.when(ix == nx - 1)
    def _():
        for it in range(ITERS):
            for c in range(CHUNKS):
                ur[it, c, 1] = jnp.zeros(ur.shape[3:], ur.dtype)

    order_copy.wait()
    for p in range(3):
        base = p * pair_w
        x = jnp.broadcast_to(order_ref[:, base:base + pair_w], (8, pair_w))
        turned = pltpu.roll(x, pair_w - 64, 1)
        low = lax.broadcasted_iota(jnp.int32, (8, 128), 1) < 64
        order[:, base:base + 256] = x[:, :256]
        order[:, base + 256:base + 512] = turned[:, 256:512]
        order[:, base + 512:base + pair_w] = jnp.where(low, x[:, 256:384], x[:, 512:])
    order[:, nf:] = jnp.broadcast_to(order_ref[:, nf:], (8, ncorn))
    step_p = 64

    def build(b, carry):
        base = pl.multiple_of(b * step_p, step_p)
        row = lax.broadcasted_iota(jnp.int32, (step_p, n), 0) + base
        perm[pl.ds(base, step_p), :] = jnp.where(row == order[0:1, :], 1.0, 0.0).astype(BF16)
        return carry

    lax.fori_loop(0, n // step_p, build, 0)
    ids_copy.wait()
    ids = ids_ref[...]
    slot = ids // (ncorn // 4)
    moved = jnp.where(slot == 1, 2, jnp.where(slot == 2, 1, slot))
    ids = moved * (ncorn // 4) + lax.rem(ids, ncorn // 4)
    place = jnp.where(lax.broadcasted_iota(jnp.int32, (ncorn, ncorn), 0) == ids, 1.0, 0.0).astype(BF16)
    cperm[...] = dot_nt(perm[:, nf:], place).astype(BF16)

    def build_t(b0, b1):
        eye = (lax.broadcasted_iota(jnp.int32, (128, 128), 0)
               == lax.broadcasted_iota(jnp.int32, (128, 128), 1))

        def body(b, carry):
            base = pl.multiple_of(b * 128, 128)
            part = order[0:1, pl.ds(base, 128)].astype(F32)
            col = jnp.sum(jnp.where(eye, part, 0.0), axis=1, keepdims=True).astype(jnp.int32)
            hit = lax.broadcasted_iota(jnp.int32, (128, n), 1) == col
            permt[pl.ds(base, 128), :] = jnp.where(hit, 1.0, 0.0).astype(BF16)
            return carry

        lax.fori_loop(b0, b1, body, 0)

    lane = lax.broadcasted_iota(jnp.int32, (R, 128), 1)
    inv_low = jnp.where(ix == nx - 1, 0.5, 0.25).astype(F32)
    inv_high = jnp.where(ix == 0, 0.5, 0.25).astype(F32)
    entries = ndev * ncorn

    def rs(c):
        return slice(c * R, (c + 1) * R)

    def field(it, c):
        for k in range(nch):
            if it == 0 and c == 0:
                flex_copy(k).wait()
            s = slice(k * cw, (k + 1) * cw)
            f = dot(loads_ref[rs(c), :] if it == 0 else rhs[rs(c), :], flex[:, s])
            fld[rs(c), s] = f
            hi, lo = split(f)
            fhi[rs(c), s] = hi
            if it == 0:
                flo[rs(c), s] = lo

    steps = (-1, 1) if ny > 2 else (1,)
    ky = len(steps)

    def y_copy(it, c, k):
        return pltpu.make_async_remote_copy(
            src_ref=cs.at[it, c], dst_ref=cr.at[it, c, k], send_sem=csend.at[it, c, k],
            recv_sem=crecv.at[it, c, k],
            device_id=(ix, lax.rem(iy + steps[k] + ny, ny)), device_id_type=MESH)

    def corners(it, c):
        cs[it, c] = dot(fhi[rs(c), :], cperm[...]) + dot(flo[rs(c), :], cperm[...])

    def face_copy(it, c, r):
        return pltpu.make_async_remote_copy(
            src_ref=tb.at[it, c, r], dst_ref=rv.at[it, c, r], send_sem=tsend.at[it, c, r],
            recv_sem=trecv.at[it, c, r], device_id=partners[r][1], device_id_type=MESH)

    def on(it, c, r, action):
        if partners[r][0] is None:
            action(face_copy(it, c, r))
        else:
            @pl.when(partners[r][0])
            def _():
                action(face_copy(it, c, r))

    def make_pair(it, c, p):
        base = p * pair_w
        t = dot(fhi[rs(c), :], perm[:, base:base + pair_w])
        for q in (0, 1):
            r = 2 * p + q
            tb[it, c, r, :R, :] = t[:, q * 256:q * 256 + 128].astype(BF16)
            tb[it, c, r, R:2 * R, :] = t[:, q * 256 + 128:q * 256 + 256].astype(BF16)
            tb[it, c, r, 2 * R:, :] = fold(t[:, 512:], q == 0).astype(BF16)

    def send(it, c, *faces):
        for r in faces:
            on(it, c, r, lambda d: d.start())

    def side_copy(it, c, k, j):
        to = jnp.clip(ix + 1 if k == 0 else ix - 1, 0, nx - 1)
        toy = iy if j == 0 else lax.rem(iy + steps[j - 1] + ny, ny)
        return pltpu.make_async_remote_copy(
            src_ref=us.at[it, c, k], dst_ref=ur.at[it, c, k, j], send_sem=usend.at[it, c, k, j],
            recv_sem=urecv.at[it, c, k, j], device_id=(to, toy), device_id_type=MESH)

    def on_sides(it, c, action, arriving):
        for k in range(2):
            @pl.when((ix > 0) if (k == 0) == arriving else (ix < nx - 1))
            def _():
                for j in range(1 + ky):
                    action(side_copy(it, c, k, j))

    def send_corners(it, c):
        us[it, c, 0] = fold(cs[it, c], True).astype(us.dtype)
        us[it, c, 1] = fold(cs[it, c], False).astype(us.dtype)
        on_sides(it, c, lambda d: d.start(), False)
        for k in range(ky):
            y_copy(it, c, k).start()

    def residual(it, c):
        for k in range(ky):
            y_copy(it, c, k).wait_recv()
        on_sides(it, c, lambda d: d.wait_recv(), True)

        def column(j):
            own = cs[it, c] if j == 0 else cr[it, c, j - 1]
            return own + unfold(ur[it, c, 1, j].astype(F32), ur[it, c, 0, j].astype(F32))

        cross = column(0) + jnp.where(lax.rem(lane, 64) < 32, pltpu.roll(column(1), 96, 1), pltpu.roll(column(ky), 32, 1))
        resid = cs[it, c] - cross * jnp.where(lane < 64, inv_low, inv_high)
        res[c] = resid
        z = jnp.concatenate([resid * resid, jnp.zeros((-R % 128, 128), F32)], axis=0)
        sq[it, c] = jnp.sum(z.T, axis=0, keepdims=True)

        def spread(k, carry):
            pltpu.make_async_remote_copy(
                src_ref=sq.at[it, c], dst_ref=sr.at[it, c, ndev - 1 - k], send_sem=ssend.at[it, c],
                recv_sem=srecv.at[it, c], device_id=peer(k), device_id_type=MESH).start()
            return carry

        lax.fori_loop(1, ndev, spread, 0)

    def own_part(it, c):
        for k in range(nch):
            s = slice(k * cw, (k + 1) * cw)
            m = cmask[:, s] * fld[rs(c), s]
            mult[rs(c), s] = m if it == 0 else mult[rs(c), s] + m

    def finish(it, c):
        for p in BACK:
            for q in (0, 1):
                on(it, c, 2 * p + q, lambda d: d.wait_recv())
            tails = []
            for q in (0, 1):
                r = 2 * p + q
                base = p * pair_w + q * 256
                xb[:, base:base + 128] = rv[it, c, r, :R, :]
                xb[:, base + 128:base + 256] = rv[it, c, r, R:2 * R, :]
                tails.append(rv[it, c, r, 2 * R:, :].astype(F32))
            xb[:, p * pair_w + 512:(p + 1) * pair_w] = unfold(*tails).astype(BF16)
            if p < 2:
                w = slice(pair_w, nf) if p else slice(0, pair_w)
                for k in range(nch):
                    s = slice(k * cw, (k + 1) * cw)
                    mult[rs(c), s] += -RHO * dot(xb[:, w], permt[w, s])
        pltpu.make_async_copy(sr.at[it, c], sr.at[it, c], srecv.at[it, c]).wait()
        total = sq[it, c] + jnp.sum(sr[it, c], axis=0)
        scale = RHO_CORNER / jnp.sqrt(total / entries + EPS)
        grid = jnp.broadcast_to(scale, (128, R + -R % 128)).T[:R]
        hi, lo = split(res[c] * grid)
        both = jnp.concatenate([hi, lo], axis=1)
        for k in range(nch):
            s = slice(k * cw, (k + 1) * cw)
            cp = cpermt[:, s]
            m = mult[rs(c), s] + dot(both, jnp.concatenate([cp, cp], axis=0))
            mult[rs(c), s] = m
            if it < ITERS - 1:
                rhs[rs(c), s] = (loads_ref[rs(c), s].astype(F32) - m).astype(BF16)

    loads_copy.wait()
    c = 0
    for it in range(ITERS):
        if it > 0:
            cs[it, c] = dot(rhs[...], fcol[...])
            send_corners(it, c)
        field(it, c)
        if it == 0:
            corners(it, c)
            pl.semaphore_wait(barrier, ndev - 1)
            send_corners(it, c)
        make_pair(it, c, 2)
        send(it, c, 4, 5)
        make_pair(it, c, 1)
        send(it, c, 2)
        make_pair(it, c, 0)
        send(it, c, 0)
        if it == 0:
            build_t(0, n // 128)
            ct = dot(place, permt[nf:, :])
            cpermt[...] = ct.astype(BF16)
            cmask[...] = RHO * (1.0 - jnp.sum(ct, axis=0, keepdims=True))
        own_part(it, c)
        residual(it, c)
        send(it, c, 1, 3)
        if it == 0:
            def corner_columns(b, carry):
                base = pl.multiple_of(b * 512, 512)
                fcol[pl.ds(base, 512), :] = dot(flex[pl.ds(base, 512), :], cperm[...]).astype(BF16)
                return carry

            lax.fori_loop(0, n // 512, corner_columns, 0)
        finish(it, c)

    for it in range(ITERS):
        for c in range(CHUNKS):
            for r in range(6):
                on(it, c, r, lambda d: d.wait_send())
            for k in range(ky):
                y_copy(it, c, k).wait_send()

            on_sides(it, c, lambda d: d.wait_send(), False)
            pltpu.make_async_copy(sr.at[it, c], sr.at[it, c], ssend.at[it, c]).wait()


def store(field, mult, field_hbm, mult_hbm, sem):
    copies = [pltpu.make_async_copy(field, field_hbm, sem.at[0]), pltpu.make_async_copy(mult, mult_hbm, sem.at[1])]
    for c in copies:
        c.start()
    for c in copies:
        c.wait()


def local(nx, ny, flexibility, loads, dof_order, coarse_ids):
    flex = flexibility[0, 0]
    load = loads[0, 0]
    ids = coarse_ids[0]
    rows, n = load.shape
    corners = ids.shape[1]
    face = (n - corners) // 6
    ndev = nx * ny
    R = rows // CHUNKS
    trace_rows = R * face // 128
    vm = pl.BlockSpec(memory_space=pltpu.VMEM)
    hbm = pl.BlockSpec(memory_space=pltpu.HBM)
    sems = pltpu.SemaphoreType.DMA
    ky = 2 if ny > 2 else 1
    out = jax.ShapeDtypeStruct((rows, n), F32)
    ic = (ITERS, CHUNKS)
    field, mult = pl.pallas_call(
        functools.partial(kernel, nx, ny),
        out_shape=(out, out),
        in_specs=[hbm, hbm, hbm, hbm],
        out_specs=(vm, vm),
        scratch_shapes=[
            pltpu.VMEM((1, n), jnp.int32), pltpu.VMEM((1, corners), jnp.int32), pltpu.VMEM((rows, n), BF16),
            pltpu.VMEM((8, n), jnp.int32),
            pltpu.VMEM((n, n), BF16), pltpu.VMEM((n, n), BF16), pltpu.VMEM((n, n), BF16),
            pltpu.VMEM((n, corners), BF16), pltpu.VMEM((corners, n), BF16),
            pltpu.VMEM((rows, n), BF16), pltpu.VMEM((rows, n), BF16), pltpu.VMEM((rows, n), BF16),
            pltpu.VMEM((1, n), F32), pltpu.VMEM((R, 6 * face), BF16), pltpu.VMEM((n, corners), BF16),
            pltpu.VMEM(ic + (6, trace_rows, 128), BF16), pltpu.VMEM(ic + (6, trace_rows, 128), BF16),
            pltpu.VMEM(ic + (R, 128), F32), pltpu.VMEM(ic + (ky, R, 128), F32),
            pltpu.VMEM(ic + (2, R // 2, 128), SIDE), pltpu.VMEM(ic + (2, 1 + ky, R // 2, 128), SIDE),
            pltpu.VMEM(ic + (1, R + -R % 128), F32), pltpu.VMEM(ic + (ndev - 1, 1, R + -R % 128), F32),
            pltpu.VMEM((CHUNKS, R, 128), F32),
            sems((3,)), sems((2,)), sems(ic + (6,)), sems(ic + (6,)), sems(ic + (ky,)), sems(ic + (ky,)),
            sems(ic + (2, 1 + ky)), sems(ic + (2, 1 + ky)), sems(ic), sems(ic),
        ],
        compiler_params=pltpu.CompilerParams(
            collective_id=0, has_side_effects=True, vmem_limit_bytes=48 * 1024 * 1024),
    )(*(pltpu.with_memory_space_constraint(x, pltpu.HBM) for x in (dof_order[0], ids, load, flex)))
    field, mult = pl.pallas_call(
        store,
        out_shape=(out, out),
        in_specs=[vm, vm],
        out_specs=(hbm, hbm),
        scratch_shapes=[sems((2,))],
        compiler_params=pltpu.CompilerParams(has_side_effects=True, vmem_limit_bytes=1024 * 1024),
    )(field, mult)
    return (field[None, None], mult[None, None])


def solution(mesh):
    nx, ny = mesh.shape["gx"], mesh.shape["gy"]
    placed = (
        P("gx", "gy", None, None),
        P("gx", "gy", None, None),
        P("gx", "gy", None),
        P("gx", "gy", None),
    )
    return jax.shard_map(
        functools.partial(local, nx, ny),
        mesh=mesh,
        in_specs=placed,
        out_specs=(P("gx", "gy", None, None), P("gx", "gy", None, None)),
        check_vma=False,
    )
```

```python
import functools
import jax
import jax.numpy as jnp
from jax import lax
from jax.experimental import pallas as pl
from jax.experimental.pallas import tpu as pltpu
from jax.sharding import PartitionSpec as P

ITERS = 2
CHUNKS = 1
RHO = 0.2
RHO_CORNER = 0.5
EPS = 1e-06
MESH = pl.DeviceIdType.MESH
ROUNDS = ((0, 1, 0), (0, 1, 1), (1, 1, 0), (1, 1, 1), (0, 2, 0), (0, 2, 2))
BACK = (2, 1, 0)
F32 = jnp.float32
BF16 = jnp.bfloat16
SIDE = F32


def dot(a, b):
    return jnp.dot(a, b, preferred_element_type=F32)


def dot_nt(a, b):
    return lax.dot_general(a, b, (((1,), (1,)), ((), ())), preferred_element_type=F32)


def split(x):
    hi = x.astype(BF16)
    return hi, (x - hi.astype(F32)).astype(BF16)


def fold(x, low):
    h = x.shape[0] // 2
    lane = lax.broadcasted_iota(jnp.int32, (h, 128), 1)
    top, bottom = x[:h], x[h:]
    if low:
        return jnp.where(lane < 64, top, pltpu.roll(bottom, 64, 1))
    return jnp.where(lane < 64, pltpu.roll(top, 64, 1), bottom)


def unfold(low, high):
    h = low.shape[0]
    lane = lax.broadcasted_iota(jnp.int32, (h, 128), 1)
    top = jnp.where(lane < 64, low, pltpu.roll(high, 64, 1))
    bottom = jnp.where(lane < 64, pltpu.roll(low, 64, 1), high)
    return jnp.concatenate([top, bottom], axis=0)


def kernel(nx, ny, order_hbm, ids_hbm, loads_hbm, flex_hbm, fld, mult, permt, cpermt, xb, both_ref,
           order_ref, ids_ref, loads_ref,
           order, flex, perm, cperm, fhi, flo, rhs, cmask, fcol,
           tb, rv, cs, cr, us, ur, sq, sr, res,
           in_sem, flex_sem, tsend, trecv, csend, crecv, usend, urecv, ssend, srecv):
    rows, n = loads_ref.shape
    face = (n - 128) // 6
    pair_w = 2 * face
    ncorn = ids_ref.shape[1]
    nf = 6 * face
    R = rows // CHUNKS
    h = R // 2
    ix, iy = lax.axis_index("gx"), lax.axis_index("gy")
    ndev = nx * ny
    me = ix * ny + iy
    nch = flex_sem.shape[0]
    cw = n // nch

    order_copy = pltpu.make_async_copy(order_hbm, order_ref, in_sem.at[0])
    ids_copy = pltpu.make_async_copy(ids_hbm, ids_ref, in_sem.at[1])
    loads_copy = pltpu.make_async_copy(loads_hbm, loads_ref, in_sem.at[2])
    order_copy.start()
    ids_copy.start()
    loads_copy.start()

    def flex_copy(c):
        s = pl.ds(c * cw, cw)
        return pltpu.make_async_copy(flex_hbm.at[:, s], flex.at[:, s], flex_sem.at[c])

    for c in range(nch):
        flex_copy(c).start()

    def peer(k):
        p = lax.rem(me + k, ndev)
        return (p // ny, lax.rem(p, ny))

    barrier = pltpu.get_barrier_semaphore()

    def greet(k, carry):
        pl.semaphore_signal(barrier, inc=1, device_id=peer(k), device_id_type=MESH)
        return carry

    lax.fori_loop(1, ndev, greet, 0)

    partners = []
    for axis, dist, off in ROUNDS:
        idx = ix if axis == 0 else iy
        count = nx if axis == 0 else ny
        lower = lax.rem((idx - off + 2 * dist) // dist, 2) == 0
        to = jnp.where(lower, idx + dist, idx - dist)
        if axis == 0:
            partners.append((jnp.logical_and(to >= 0, to < count), (jnp.clip(to, 0, count - 1), iy)))
        else:
            partners.append((None, (ix, lax.rem(to + count, count))))

    for r in range(6):
        present = partners[r][0]
        if present is not None:
            @pl.when(jnp.logical_not(present))
            def _():
                for it in range(ITERS):
                    for c in range(CHUNKS):
                        rv[it, c, r] = jnp.zeros(rv.shape[3:], BF16)

    @pl.when(ix == 0)
    def _():
        for it in range(ITERS):
            for c in range(CHUNKS):
                ur[it, c, 0] = jnp.zeros(ur.shape[3:], ur.dtype)

    @pl.when(ix == nx - 1)
    def _():
        for it in range(ITERS):
            for c in range(CHUNKS):
                ur[it, c, 1] = jnp.zeros(ur.shape[3:], ur.dtype)

    order_copy.wait()
    for p in range(3):
        base = p * pair_w
        x = jnp.broadcast_to(order_ref[:, base:base + pair_w], (8, pair_w))
        turned = pltpu.roll(x, pair_w - 64, 1)
        low = lax.broadcasted_iota(jnp.int32, (8, 128), 1) < 64
        order[:, base:base + 256] = x[:, :256]
        order[:, base + 256:base + 512] = turned[:, 256:512]
        order[:, base + 512:base + pair_w] = jnp.where(low, x[:, 256:384], x[:, 512:])
    order[:, nf:] = jnp.broadcast_to(order_ref[:, nf:], (8, ncorn))
    step_p = 64

    def build(b, carry):
        base = pl.multiple_of(b * step_p, step_p)
        row = lax.broadcasted_iota(jnp.int32, (step_p, n), 0) + base
        perm[pl.ds(base, step_p), :] = jnp.where(row == order[0:1, :], 1.0, 0.0).astype(BF16)
        return carry

    lax.fori_loop(0, n // step_p, build, 0)
    ids_copy.wait()
    ids = ids_ref[...]
    slot = ids // (ncorn // 4)
    moved = jnp.where(slot == 1, 2, jnp.where(slot == 2, 1, slot))
    ids = moved * (ncorn // 4) + lax.rem(ids, ncorn // 4)
    place = jnp.where(lax.broadcasted_iota(jnp.int32, (ncorn, ncorn), 0) == ids, 1.0, 0.0).astype(BF16)
    cperm[...] = dot_nt(perm[:, nf:], place).astype(BF16)

    def build_t(b0, b1):
        eye = (lax.broadcasted_iota(jnp.int32, (128, 128), 0)
               == lax.broadcasted_iota(jnp.int32, (128, 128), 1))

        def body(b, carry):
            base = pl.multiple_of(b * 128, 128)
            part = order[0:1, pl.ds(base, 128)].astype(F32)
            col = jnp.sum(jnp.where(eye, part, 0.0), axis=1, keepdims=True).astype(jnp.int32)
            hit = lax.broadcasted_iota(jnp.int32, (128, n), 1) == col
            permt[pl.ds(base, 128), :] = jnp.where(hit, 1.0, 0.0).astype(BF16)
            return carry

        lax.fori_loop(b0, b1, body, 0)

    lane = lax.broadcasted_iota(jnp.int32, (R, 128), 1)
    inv_low = jnp.where(ix == nx - 1, 0.5, 0.25).astype(F32)
    inv_high = jnp.where(ix == 0, 0.5, 0.25).astype(F32)
    entries = ndev * ncorn

    def rs(c):
        return slice(c * R, (c + 1) * R)

    def field(it, c):
        for k in range(nch):
            if it == 0 and c == 0:
                flex_copy(k).wait()
            s = slice(k * cw, (k + 1) * cw)
            f = dot(loads_ref[rs(c), :] if it == 0 else rhs[rs(c), :], flex[:, s])
            fld[rs(c), s] = f
            hi, lo = split(f)
            fhi[rs(c), s] = hi
            if it == 0:
                flo[rs(c), s] = lo

    steps = (-1, 1) if ny > 2 else (1,)
    ky = len(steps)

    def y_copy(it, c, k):
        return pltpu.make_async_remote_copy(
            src_ref=cs.at[it, c], dst_ref=cr.at[it, c, k], send_sem=csend.at[it, c, k],
            recv_sem=crecv.at[it, c, k],
            device_id=(ix, lax.rem(iy + steps[k] + ny, ny)), device_id_type=MESH)

    def corners(it, c):
        cs[it, c] = dot(fhi[rs(c), :], cperm[...]) + dot(flo[rs(c), :], cperm[...])

    def face_copy(it, c, r):
        return pltpu.make_async_remote_copy(
            src_ref=tb.at[it, c, r], dst_ref=rv.at[it, c, r], send_sem=tsend.at[it, c, r],
            recv_sem=trecv.at[it, c, r], device_id=partners[r][1], device_id_type=MESH)

    def on(it, c, r, action):
        if partners[r][0] is None:
            action(face_copy(it, c, r))
        else:
            @pl.when(partners[r][0])
            def _():
                action(face_copy(it, c, r))

    def make_pair(it, c, p):
        base = p * pair_w
        t = dot(fhi[rs(c), :], perm[:, base:base + pair_w])
        for q in (0, 1):
            r = 2 * p + q
            tb[it, c, r, :R, :] = t[:, q * 256:q * 256 + 128].astype(BF16)
            tb[it, c, r, R:2 * R, :] = t[:, q * 256 + 128:q * 256 + 256].astype(BF16)
            tb[it, c, r, 2 * R:, :] = fold(t[:, 512:], q == 0).astype(BF16)

    def send(it, c, *faces):
        for r in faces:
            on(it, c, r, lambda d: d.start())

    def side_copy(it, c, k, j):
        to = jnp.clip(ix + 1 if k == 0 else ix - 1, 0, nx - 1)
        toy = iy if j == 0 else lax.rem(iy + steps[j - 1] + ny, ny)
        return pltpu.make_async_remote_copy(
            src_ref=us.at[it, c, k], dst_ref=ur.at[it, c, k, j], send_sem=usend.at[it, c, k, j],
            recv_sem=urecv.at[it, c, k, j], device_id=(to, toy), device_id_type=MESH)

    def on_sides(it, c, action, arriving):
        for k in range(2):
            @pl.when((ix > 0) if (k == 0) == arriving else (ix < nx - 1))
            def _():
                for j in range(1 + ky):
                    action(side_copy(it, c, k, j))

    def send_corners(it, c):
        us[it, c, 0] = fold(cs[it, c], True).astype(us.dtype)
        us[it, c, 1] = fold(cs[it, c], False).astype(us.dtype)
        on_sides(it, c, lambda d: d.start(), False)
        for k in range(ky):
            y_copy(it, c, k).start()

    def residual(it, c):
        for k in range(ky):
            y_copy(it, c, k).wait_recv()
        on_sides(it, c, lambda d: d.wait_recv(), True)

        def column(j):
            own = cs[it, c] if j == 0 else cr[it, c, j - 1]
            return own + unfold(ur[it, c, 1, j].astype(F32), ur[it, c, 0, j].astype(F32))

        cross = column(0) + jnp.where(lax.rem(lane, 64) < 32, pltpu.roll(column(1), 96, 1), pltpu.roll(column(ky), 32, 1))
        resid = cs[it, c] - cross * jnp.where(lane < 64, inv_low, inv_high)
        res[c] = resid
        z = jnp.concatenate([resid * resid, jnp.zeros((-R % 128, 128), F32)], axis=0)
        sq[it, c] = jnp.sum(z.T, axis=0, keepdims=True)

        def spread(t, carry):
            p = jnp.where(2 * me < ndev, ndev - 1 - t, t)
            p = jnp.where(2 * me < ndev, jnp.where(p <= me, p - 1, p), jnp.where(p >= me, p + 1, p))
            k = lax.rem(p - me + ndev, ndev)
            pltpu.make_async_remote_copy(
                src_ref=sq.at[it, c], dst_ref=sr.at[it, c, ndev - 1 - k], send_sem=ssend.at[it, c],
                recv_sem=srecv.at[it, c], device_id=(p // ny, lax.rem(p, ny)), device_id_type=MESH).start()
            return carry

        lax.fori_loop(0, ndev - 1, spread, 0)

    def own_part(it, c):
        for k in range(nch):
            s = slice(k * cw, (k + 1) * cw)
            m = cmask[:, s] * fld[rs(c), s]
            mult[rs(c), s] = m if it == 0 else mult[rs(c), s] + m

    def finish(it, c):
        for p in BACK:
            for q in (0, 1):
                on(it, c, 2 * p + q, lambda d: d.wait_recv())
            tails = []
            for q in (0, 1):
                r = 2 * p + q
                base = p * pair_w + q * 256
                xb[:, base:base + 128] = rv[it, c, r, :R, :]
                xb[:, base + 128:base + 256] = rv[it, c, r, R:2 * R, :]
                tails.append(rv[it, c, r, 2 * R:, :].astype(F32))
            xb[:, p * pair_w + 512:(p + 1) * pair_w] = unfold(*tails).astype(BF16)
            if p == 1 or (p == 0 and it < ITERS - 1):
                w = slice(pair_w, nf) if p else slice(0, pair_w)
                for k in range(nch):
                    s = slice(k * cw, (k + 1) * cw)
                    mult[rs(c), s] += -RHO * dot(xb[:, w], permt[w, s])
        pltpu.make_async_copy(sr.at[it, c], sr.at[it, c], srecv.at[it, c]).wait()
        total = sq[it, c] + jnp.sum(sr[it, c], axis=0)
        scale = RHO_CORNER / jnp.sqrt(total / entries + EPS)
        grid = jnp.broadcast_to(scale, (128, R + -R % 128)).T[:R]
        hi, lo = split(res[c] * grid)
        both = jnp.concatenate([hi, lo], axis=1)
        if it == ITERS - 1:
            both_ref[...] = both
            return
        for k in range(nch):
            s = slice(k * cw, (k + 1) * cw)
            cp = cpermt[:, s]
            m = mult[rs(c), s] + dot(both, jnp.concatenate([cp, cp], axis=0))
            mult[rs(c), s] = m
            if it < ITERS - 1:
                rhs[rs(c), s] = (loads_ref[rs(c), s].astype(F32) - m).astype(BF16)

    loads_copy.wait()
    c = 0
    for it in range(ITERS):
        if it > 0:
            cs[it, c] = dot(rhs[...], fcol[...])
            send_corners(it, c)
        field(it, c)
        if it == 0:
            corners(it, c)
            pl.semaphore_wait(barrier, ndev - 1)
            send_corners(it, c)
        make_pair(it, c, 2)
        send(it, c, 4, 5)
        make_pair(it, c, 1)
        send(it, c, 2)
        make_pair(it, c, 0)
        send(it, c, 0)
        if it == 0:
            build_t(0, n // 128)
            ct = dot(place, permt[nf:, :])
            cpermt[...] = ct.astype(BF16)
            cmask[...] = RHO * (1.0 - jnp.sum(ct, axis=0, keepdims=True))
        own_part(it, c)
        residual(it, c)
        send(it, c, 1, 3)
        if it == 0:
            def corner_columns(b, carry):
                base = pl.multiple_of(b * 512, 512)
                fcol[pl.ds(base, 512), :] = dot(flex[pl.ds(base, 512), :], cperm[...]).astype(BF16)
                return carry

            lax.fori_loop(0, n // 512, corner_columns, 0)
        finish(it, c)

    for it in range(ITERS):
        for c in range(CHUNKS):
            for r in range(6):
                on(it, c, r, lambda d: d.wait_send())
            for k in range(ky):
                y_copy(it, c, k).wait_send()

            on_sides(it, c, lambda d: d.wait_send(), False)
            pltpu.make_async_copy(sr.at[it, c], sr.at[it, c], ssend.at[it, c]).wait()


def store(field, mult, permt, cpermt, xb, both, field_hbm, mult_hbm, total, sem):
    n = field.shape[1]
    pair_w = (n - cpermt.shape[0]) // 3
    blocks = sem.shape[0] - 1
    copies = [pltpu.make_async_copy(field, field_hbm, sem.at[blocks])]
    copies[0].start()
    for k in range(blocks):
        s = slice(k * (n // blocks), (k + 1) * (n // blocks))
        cp = cpermt[:, s]
        total[:, s] = mult[:, s] + (dot(both[...], jnp.concatenate([cp, cp], axis=0))
                                    - RHO * dot(xb[:, :pair_w], permt[:pair_w, s]))
        copies.append(pltpu.make_async_copy(total.at[:, s], mult_hbm.at[:, s], sem.at[k]))
        copies[-1].start()
    for c in copies:
        c.wait()


def local(nx, ny, flexibility, loads, dof_order, coarse_ids):
    flex = flexibility[0, 0]
    load = loads[0, 0]
    ids = coarse_ids[0]
    rows, n = load.shape
    corners = ids.shape[1]
    face = (n - corners) // 6
    ndev = nx * ny
    R = rows // CHUNKS
    trace_rows = R * face // 128
    vm = pl.BlockSpec(memory_space=pltpu.VMEM)
    hbm = pl.BlockSpec(memory_space=pltpu.HBM)
    sems = pltpu.SemaphoreType.DMA
    ky = 2 if ny > 2 else 1
    out = jax.ShapeDtypeStruct((rows, n), F32)
    ic = (ITERS, CHUNKS)
    field, mult, *rest = pl.pallas_call(
        functools.partial(kernel, nx, ny),
        out_shape=(out, out, jax.ShapeDtypeStruct((n, n), BF16), jax.ShapeDtypeStruct((corners, n), BF16),
                   jax.ShapeDtypeStruct((R, 6 * face), BF16), jax.ShapeDtypeStruct((R, 2 * corners), BF16)),
        in_specs=[hbm, hbm, hbm, hbm],
        out_specs=(vm,) * 6,
        scratch_shapes=[
            pltpu.VMEM((1, n), jnp.int32), pltpu.VMEM((1, corners), jnp.int32), pltpu.VMEM((rows, n), BF16),
            pltpu.VMEM((8, n), jnp.int32),
            pltpu.VMEM((n, n), BF16), pltpu.VMEM((n, n), BF16),
            pltpu.VMEM((n, corners), BF16),
            pltpu.VMEM((rows, n), BF16), pltpu.VMEM((rows, n), BF16), pltpu.VMEM((rows, n), BF16),
            pltpu.VMEM((1, n), F32), pltpu.VMEM((n, corners), BF16),
            pltpu.VMEM(ic + (6, trace_rows, 128), BF16), pltpu.VMEM(ic + (6, trace_rows, 128), BF16),
            pltpu.VMEM(ic + (R, 128), F32), pltpu.VMEM(ic + (ky, R, 128), F32),
            pltpu.VMEM(ic + (2, R // 2, 128), SIDE), pltpu.VMEM(ic + (2, 1 + ky, R // 2, 128), SIDE),
            pltpu.VMEM(ic + (1, R + -R % 128), F32), pltpu.VMEM(ic + (ndev - 1, 1, R + -R % 128), F32),
            pltpu.VMEM((CHUNKS, R, 128), F32),
            sems((3,)), sems((2,)), sems(ic + (6,)), sems(ic + (6,)), sems(ic + (ky,)), sems(ic + (ky,)),
            sems(ic + (2, 1 + ky)), sems(ic + (2, 1 + ky)), sems(ic), sems(ic),
        ],
        compiler_params=pltpu.CompilerParams(
            collective_id=0, has_side_effects=True, vmem_limit_bytes=38 * 1024 * 1024),
    )(*(pltpu.with_memory_space_constraint(x, pltpu.HBM) for x in (dof_order[0], ids, load, flex)))
    field, mult = pl.pallas_call(
        store,
        out_shape=(out, out),
        in_specs=[vm] * 6,
        out_specs=(hbm, hbm),
        scratch_shapes=[pltpu.VMEM((rows, n), F32), sems((5,))],
        compiler_params=pltpu.CompilerParams(has_side_effects=True, vmem_limit_bytes=8 * 1024 * 1024),
    )(field, mult, *rest)
    return (field[None, None], mult[None, None])


def solution(mesh):
    nx, ny = mesh.shape["gx"], mesh.shape["gy"]
    placed = (
        P("gx", "gy", None, None),
        P("gx", "gy", None, None),
        P("gx", "gy", None),
        P("gx", "gy", None),
    )
    return jax.shard_map(
        functools.partial(local, nx, ny),
        mesh=mesh,
        in_specs=placed,
        out_specs=(P("gx", "gy", None, None), P("gx", "gy", None, None)),
        check_vma=False,
    )
```
